512 devices in a mesh: expert: 128 (over y, z, core), dp: 4 (over x).
Axes of the slice: x: 4, y: 8, z: 8, core: 2. Of those that a mesh axis runs over, the one named last changes fastest.
Arguments:
- hidden: bfloat16 [128, 4, 256, 1024], P('expert', 'dp'), may hold values from -6 to 6
- w_down: bfloat16 [128, 1024, 3584], P('expert', 'dp'), may hold values from -0.1875 to 0.1875
- expert_ids: int32 [4, 2048, 8], P('dp', 'expert'), may hold values from 0 to 127, all different within a row; in each aligned block of 16 rows (0 to 15, 16 to 31, ..., all dimensions but the last counted through in order) at most 2 rows name the same one
- route_weights: float32 [4, 2048, 8], P('dp', 'expert'), may hold values from 0.1 to 0.6
- grad_out: bfloat16 [4, 2048, 3584], P('dp', 'expert'), may hold values from -6 to 6
Outputs:
- mixed: bfloat16 [4, 2048, 3584], P('dp', 'expert')
- d_hidden: bfloat16 [128, 4, 256, 1024], P('expert', 'dp')
- d_w_down: bfloat16 [128, 1024, 3584], P('expert', 'dp')
- d_route: float32 [4, 2048, 8], P('dp', 'expert')
The draws below stay inside these ranges and needn't reach their ends.
Inputs may be any that keep to these rules, and one draw needn't show every extreme that they name: `expert_ids`: among the 16 tokens of one device no expert is chosen more than 2 times, and some expert is chosen exactly 2 times; the 8 choices of a token are distinct.
All inputs are finite; a program needn't handle non-finite values.
Results may differ from the reference program's by a relative error of at most 0.0085.
Values may be sent and summed in bfloat16 or wider, within the bound.
A program may use at most 128 MiB of HBM per device.

```python
import math
import jax
import jax.numpy as jnp
import numpy as np
from jax import lax

D = 3584
H = 1024
TOPK = 8
TOK_DEV = 16
E = 128
C = 2
TOKENS = 2048
N_EXPERT = 128
N_DP = 4


def shard_levels(rng, extent, cuts, least, top_value):
    gain = 1.0
    for axis_at, parts in cuts:
        steps = jax.random.uniform(jax.random.fold_in(jax.random.fold_in(rng, 6), axis_at), (parts,), jnp.float32, least / len(cuts), top_value / len(cuts))
        gain = gain * jnp.repeat(jnp.exp(steps), extent[axis_at] // parts).reshape((-1,) + (1,) * (len(extent) - 1 - axis_at))
    return gain


def deal_out(rng, own, number, rows, amount, top, reach, skew):
    ranking = jax.random.permutation(rng, amount)
    packed, ordinary = load_shares(amount, rows * top, reach, skew, True), load_shares(amount, rows * top, reach, skew, False)
    places = jnp.arange(amount)

    def named(tallies, rotation):
        used = int((tallies > 0).sum())
        fixed = max(1, used // 4)
        moved = fixed + (places - fixed + rotation * (used - fixed)) % max(1, amount - fixed)
        return jnp.zeros((amount,), jnp.int32).at[ranking[jnp.where(places < fixed, places, moved)]].set(jnp.asarray(tallies, jnp.int32))

    tallies = jnp.where(number % 4 == 0, named(packed, number // 4), named(ordinary, number - number // 4 - 1))
    mixed = jax.random.permutation(jax.random.fold_in(own, 3), amount)
    source_of, receiver = mixed[0:amount // 2 * 2:2], mixed[1:amount // 2 * 2:2]
    room = jnp.minimum(tallies[source_of] - 1, reach - tallies[receiver]) // 2
    room = jnp.where((source_of == ranking[0]) | (receiver == ranking[0]) | (tallies[receiver] == 0), 0, jnp.maximum(room, 0))
    moved = jax.random.randint(jax.random.fold_in(own, 4), (amount // 2,), 0, 1 << 20) % (room + 1)
    tallies = tallies.at[source_of].add(-moved).at[receiver].add(moved)
    labels = jnp.searchsorted(jnp.cumsum(tallies), jnp.arange(rows * top), side="right").astype(jnp.int32)
    listing = labels.reshape(top, rows).T
    listing = listing[jax.random.permutation(jax.random.fold_in(own, 1), rows)]
    rotation = jax.random.randint(jax.random.fold_in(own, 2), (rows, 1), 0, top)
    return jnp.take_along_axis(listing, (jnp.arange(top)[None, :] + rotation) % top, axis=1)


def load_shares(count, total, limit, lean, full):
    loads = [(1 << 20) // math.isqrt(rank ** lean) + 1 for rank in range(1, count + 1)]
    largest = limit if full else min(limit, max(-(-total // count), total * loads[0] // sum(loads)))
    least = 1 if total - largest >= count - 1 else 0
    counts, surplus = [largest] + [least] * (count - 1), total - largest - least * (count - 1)
    while surplus > 0:
        free = [i for i in range(1, count) if counts[i] < largest] or [i for i in range(1, count) if counts[i] < limit]
        mass, budget = sum([loads[i] for i in free]), surplus
        for i in free:
            more = min(limit - counts[i], max(1, budget * loads[i] // mass), surplus)
            counts[i] = counts[i] + more
            surplus = surplus - more
    return np.array(counts)


def centred(stream_key, extent, scale, bound, shards=(), kind=jnp.bfloat16):
    factor_of = shard_levels(stream_key, extent, shards, -0.22, 0.18) if shards else 1.0
    array = jax.random.normal(stream_key, extent, jnp.float32) * scale * factor_of
    return jnp.minimum(jnp.maximum(array, -bound), bound).astype(kind)


def setup_inputs(seed: int = 0) -> dict:
    streams_of = jax.random.split(jax.random.key(seed), 6)
    hidden = centred(streams_of[0], (E, N_DP, E * C, H), 1.0, 6.0, ((0, 128), (1, 4)))
    w_down = centred(streams_of[1], (E, H, D), H ** -0.5, 0.1875, ((0, 128), (1, 4)))
    expert_ids_keys = jax.random.split(jax.random.fold_in(streams_of[2], 1), N_DP * TOKENS // TOK_DEV)
    expert_ids_turns = jax.random.permutation(jax.random.fold_in(streams_of[2], 3), N_DP * TOKENS // TOK_DEV)
    expert_ids = jax.vmap(lambda own, number: deal_out(jax.random.fold_in(streams_of[2], 2), own, number, TOK_DEV, E, TOPK, C, 2))(expert_ids_keys, expert_ids_turns).reshape((N_DP, TOKENS, TOPK))
    route_weights = jnp.clip(0.1 + 0.5 * jax.random.uniform(streams_of[3], (N_DP, TOKENS, TOPK), jnp.float32) ** shard_levels(streams_of[3], (N_DP, TOKENS, TOPK), ((0, 4), (1, 128)), -0.2, 0.2), 0.1, 0.6)
    grad_out = centred(streams_of[4], (N_DP, TOKENS, D), 1.0, 6.0, ((0, 4), (1, 128)))
    return dict(hidden=hidden, w_down=w_down, expert_ids=expert_ids, route_weights=route_weights, grad_out=grad_out)


def slot_ranks(choices):
    flat = choices.reshape(-1)
    onehot = (flat[:, None] == jnp.arange(N_EXPERT, dtype=jnp.int32)[None, :]).astype(jnp.int32)
    earlier = jnp.cumsum(onehot, axis=0) - onehot
    return jnp.sum(earlier * onehot, axis=1).astype(jnp.int32).reshape(choices.shape)


def forward_expert(pair):
    acts, weight = pair
    flat = acts.reshape(-1, H)
    result = jnp.dot(flat, weight, preferred_element_type=jnp.float32).astype(jnp.bfloat16)
    return result.reshape(N_DP, N_EXPERT * C, D)


def backward_expert(triple):
    acts, weight, grads = triple
    flat_acts = acts.reshape(-1, H)
    flat_grads = grads.reshape(-1, D)
    d_acts = jnp.einsum("rd,hd->rh", flat_grads, weight, preferred_element_type=jnp.float32).astype(jnp.bfloat16)
    d_weight = jnp.einsum("rh,rd->hd", flat_acts, flat_grads, preferred_element_type=jnp.float32).astype(jnp.bfloat16)
    return d_acts.reshape(acts.shape), d_weight


def reference(hidden, w_down, expert_ids, route_weights, grad_out):
    choices = expert_ids.reshape(N_DP, N_EXPERT, TOK_DEV, TOPK)
    ranks = jax.vmap(jax.vmap(slot_ranks))(choices)
    source = jnp.arange(N_EXPERT, dtype=jnp.int32)[None, :, None, None]
    rows = (source * C + ranks).astype(jnp.int32)
    groups = jnp.broadcast_to(jnp.arange(N_DP, dtype=jnp.int32)[:, None, None, None], choices.shape)
    out_slots = lax.map(forward_expert, (hidden, w_down))
    out_pair = out_slots[choices, groups, rows].astype(jnp.float32)
    weights = route_weights.reshape(N_DP, N_EXPERT, TOK_DEV, TOPK)
    mixed = jnp.sum(weights[..., None] * out_pair, axis=3)
    cotangent = grad_out.reshape(N_DP, N_EXPERT, TOK_DEV, D).astype(jnp.float32)
    d_route = jnp.sum(cotangent[:, :, :, None, :] * out_pair, axis=-1)
    grad_pair = (weights[..., None] * cotangent[:, :, :, None, :]).astype(jnp.bfloat16)
    grad_slots = jnp.zeros((N_EXPERT, N_DP, N_EXPERT * C, D), jnp.bfloat16).at[choices, groups, rows].set(grad_pair)
    d_hidden, d_w_down = lax.map(backward_expert, (hidden, w_down, grad_slots))
    return (mixed.reshape(N_DP, TOKENS, D).astype(jnp.bfloat16), d_hidden, d_w_down, d_route.reshape(N_DP, TOKENS, TOPK))
```

```python
import jax
import jax.numpy as jnp
from jax import lax
from jax.sharding import PartitionSpec as P

CHUNKS = 2


def slot_ranks(choices, experts):
    flat = choices.reshape(-1)
    onehot = (flat[:, None] == jnp.arange(experts, dtype=jnp.int32)[None, :]).astype(jnp.int32)
    earlier = jnp.cumsum(onehot, axis=0) - onehot
    return jnp.sum(earlier * onehot, axis=1).reshape(choices.shape)


def on_device(hidden, w_down, expert_ids, route_weights, grad_out):
    experts = lax.axis_size("expert")
    groups = lax.axis_size("dp")
    assert groups == 4
    slots = hidden.shape[2] // experts
    width = w_down.shape[2]
    kpart = w_down.shape[1]
    f32, bf16 = jnp.float32, jnp.bfloat16
    d = lax.axis_index("dp")
    parity = d % 2
    half = d // 2
    mate = d + 1 - 2 * parity
    pair_a = [(i, i ^ 1) for i in range(groups)]
    pair_b = [(i, groups - 1 - i) for i in range(groups)]
    hid = hidden[0, 0]
    rows = hid.shape[0]

    def cols(x, k):
        return lax.dynamic_slice_in_dim(x, k * kpart, kpart, axis=1)

    hid_b = lax.ppermute(
        lax.dynamic_slice_in_dim(hid, (1 - half) * 2 * kpart, 2 * kpart, axis=1), "dp", pair_b
    )
    lhs_own = jnp.concatenate([cols(hid, d), cols(hid_b, parity)], axis=0)
    lhs_mate = jnp.concatenate([cols(hid, mate), cols(hid_b, 1 - parity)], axis=0)

    cw = width // CHUNKS
    w_own = w_down[0]
    w_own_c, w_mate_c, out_c = [], [], []
    for c in range(CHUNKS):
        wo = w_own[:, c * cw:(c + 1) * cw]
        wm = lax.ppermute(wo, "dp", pair_a)
        w_own_c.append(wo)
        w_mate_c.append(wm)
        part = jnp.dot(lhs_own, wo, preferred_element_type=f32) + jnp.dot(
            lhs_mate, wm, preferred_element_type=f32
        )
        got = lax.ppermute(part[rows:].astype(bf16), "dp", pair_b)
        out_c.append((part[:rows] + got.astype(f32)).astype(bf16))
    out_slots = jnp.concatenate(out_c, axis=1)

    arrived = lax.all_to_all(
        out_slots.reshape(experts, slots, width), "expert", split_axis=0, concat_axis=0, tiled=True
    )
    arrived = arrived.reshape(experts * slots, width)
    choices = expert_ids[0]
    weights = route_weights[0]
    cotangent = grad_out[0].astype(f32)
    slot_rows = choices * slots + slot_ranks(choices, experts)
    out_pair = arrived[slot_rows].astype(f32)
    mixed = jnp.einsum("tk,tkd->td", weights, out_pair)
    d_route = jnp.einsum("td,tkd->tk", cotangent, out_pair)
    grad_pair = (weights[..., None] * cotangent[:, None, :]).astype(bf16)
    outgoing = jnp.zeros((experts * slots, width), bf16)
    outgoing = outgoing.at[slot_rows.reshape(-1)].set(grad_pair.reshape(-1, width))
    mine = lax.all_to_all(
        outgoing.reshape(experts, slots, width), "expert", split_axis=0, concat_axis=0, tiled=True
    )
    g_own = mine.reshape(experts * slots, width)

    dw_c = []
    dh_own = jnp.zeros((2 * rows, kpart), f32)
    dh_mate = jnp.zeros((2 * rows, kpart), f32)
    for c in range(CHUNKS):
        go = g_own[:, c * cw:(c + 1) * cw]
        gb = lax.ppermute(go, "dp", pair_b)
        g = jnp.concatenate([go, gb], axis=0)
        q_own = jnp.einsum("rh,rd->hd", lhs_own, g, preferred_element_type=f32)
        q_mate = jnp.einsum("rh,rd->hd", lhs_mate, g, preferred_element_type=f32)
        got = lax.ppermute(q_mate.astype(bf16), "dp", pair_a)
        dw_c.append((q_own + got.astype(f32)).astype(bf16))
        dh_own = dh_own + jnp.einsum("rd,hd->rh", g, w_own_c[c], preferred_element_type=f32)
        dh_mate = dh_mate + jnp.einsum("rd,hd->rh", g, w_mate_c[c], preferred_element_type=f32)
    d_weight = jnp.concatenate(dw_c, axis=1)

    dh_own = dh_own.astype(bf16)
    dh_mate = dh_mate.astype(bf16)
    first = parity == 0
    here = jnp.where(first, jnp.concatenate([dh_own, dh_mate], axis=1),
                     jnp.concatenate([dh_mate, dh_own], axis=1))
    there = lax.ppermute(here[rows:], "dp", pair_b)
    d_hidden = jnp.where(half == 0, jnp.concatenate([here[:rows], there], axis=1),
                         jnp.concatenate([there, here[:rows]], axis=1))
    return (
        mixed.astype(bf16)[None],
        d_hidden.reshape(hidden.shape),
        d_weight[None],
        d_route[None],
    )


def solution(mesh):
    placed = (
        P("expert", "dp", None, None),
        P("expert", "dp", None),
        P("dp", "expert", None),
        P("dp", "expert", None),
        P("dp", "expert", None),
    )
    return jax.shard_map(
        on_device,
        mesh=mesh,
        in_specs=placed,
        out_specs=(
            P("dp", "expert", None),
            P("expert", "dp", None, None),
            P("expert", "dp", None),
            P("dp", "expert", None),
        ),
        check_vma=False,
    )
```

```python
import jax
import jax.numpy as jnp
from jax import lax
from jax.sharding import PartitionSpec as P

CHUNKS = 4


def slot_ranks(choices, experts):
    flat = choices.reshape(-1)
    onehot = (flat[:, None] == jnp.arange(experts, dtype=jnp.int32)[None, :]).astype(jnp.int32)
    earlier = jnp.cumsum(onehot, axis=0) - onehot
    return jnp.sum(earlier * onehot, axis=1).reshape(choices.shape)


def on_device(hidden, w_down, expert_ids, route_weights, grad_out):
    experts = lax.axis_size("expert")
    groups = lax.axis_size("dp")
    assert groups == 4
    slots = hidden.shape[2] // experts
    width = w_down.shape[2]
    kpart = w_down.shape[1]
    f32, bf16 = jnp.float32, jnp.bfloat16
    d = lax.axis_index("dp")
    parity = d % 2
    half = d // 2
    mate = d + 1 - 2 * parity
    pair_a = [(i, i ^ 1) for i in range(groups)]
    pair_b = [(i, groups - 1 - i) for i in range(groups)]
    hid = hidden[0, 0]
    rows = hid.shape[0]

    def cols(x, k):
        return lax.dynamic_slice_in_dim(x, k * kpart, kpart, axis=1)

    hid_b = lax.ppermute(
        lax.dynamic_slice_in_dim(hid, (1 - half) * 2 * kpart, 2 * kpart, axis=1), "dp", pair_b
    )
    lhs_own = jnp.concatenate([cols(hid, d), cols(hid_b, parity)], axis=0)
    lhs_mate = jnp.concatenate([cols(hid, mate), cols(hid_b, 1 - parity)], axis=0)

    cw = width // CHUNKS
    w_own = w_down[0]
    w_own_c, w_mate_c, out_c = [], [], []
    got = None
    for c in range(CHUNKS):
        wo = w_own[:, c * cw:(c + 1) * cw]
        if c:
            wo, _ = lax.optimization_barrier((wo, w_mate_c[-1]))
        wm = lax.ppermute(wo, "dp", pair_a)
        w_own_c.append(wo)
        w_mate_c.append(wm)
        part = jnp.dot(lhs_own, wo, preferred_element_type=f32) + jnp.dot(
            lhs_mate, wm, preferred_element_type=f32
        )
        send = part[rows:].astype(bf16)
        if c:
            send, _ = lax.optimization_barrier((send, got))
        got = lax.ppermute(send, "dp", pair_b)
        out_c.append((part[:rows] + got.astype(f32)).astype(bf16))
    out_slots = jnp.concatenate(out_c, axis=1)

    arrived = lax.all_to_all(
        out_slots.reshape(experts, slots, width), "expert", split_axis=0, concat_axis=0, tiled=True
    )
    arrived = arrived.reshape(experts * slots, width)
    choices = expert_ids[0]
    weights = route_weights[0]
    cotangent = grad_out[0].astype(f32)
    slot_rows = choices * slots + slot_ranks(choices, experts)
    out_pair = arrived[slot_rows].astype(f32)
    mixed = jnp.einsum("tk,tkd->td", weights, out_pair)
    d_route = jnp.einsum("td,tkd->tk", cotangent, out_pair)
    grad_pair = (weights[..., None] * cotangent[:, None, :]).astype(bf16)
    outgoing = jnp.zeros((experts * slots, width), bf16)
    outgoing = outgoing.at[slot_rows.reshape(-1)].set(grad_pair.reshape(-1, width))
    mine = lax.all_to_all(
        outgoing.reshape(experts, slots, width), "expert", split_axis=0, concat_axis=0, tiled=True
    )
    g_own = mine.reshape(experts * slots, width)

    dw_c = []
    dh_own = jnp.zeros((2 * rows, kpart), f32)
    dh_mate = jnp.zeros((2 * rows, kpart), f32)
    gb = got = None
    for c in range(CHUNKS):
        go = g_own[:, c * cw:(c + 1) * cw]
        if c:
            go, _ = lax.optimization_barrier((go, gb))
        gb = lax.ppermute(go, "dp", pair_b)
        g = jnp.concatenate([go, gb], axis=0)
        q_own = jnp.einsum("rh,rd->hd", lhs_own, g, preferred_element_type=f32)
        q_mate = jnp.einsum("rh,rd->hd", lhs_mate, g, preferred_element_type=f32)
        send = q_mate.astype(bf16)
        if c:
            send, _ = lax.optimization_barrier((send, got))
        got = lax.ppermute(send, "dp", pair_a)
        dw_c.append((q_own + got.astype(f32)).astype(bf16))
        dh_own = dh_own + jnp.einsum("rd,hd->rh", g, w_own_c[c], preferred_element_type=f32)
        dh_mate = dh_mate + jnp.einsum("rd,hd->rh", g, w_mate_c[c], preferred_element_type=f32)
    d_weight = jnp.concatenate(dw_c, axis=1)

    dh_own = dh_own.astype(bf16)
    dh_mate = dh_mate.astype(bf16)
    first = parity == 0
    here = jnp.where(first, jnp.concatenate([dh_own, dh_mate], axis=1),
                     jnp.concatenate([dh_mate, dh_own], axis=1))
    there = lax.ppermute(here[rows:], "dp", pair_b)
    d_hidden = jnp.where(half == 0, jnp.concatenate([here[:rows], there], axis=1),
                         jnp.concatenate([there, here[:rows]], axis=1))
    return (
        mixed.astype(bf16)[None],
        d_hidden.reshape(hidden.shape),
        d_weight[None],
        d_route[None],
    )


def solution(mesh):
    placed = (
        P("expert", "dp", None, None),
        P("expert", "dp", None),
        P("dp", "expert", None),
        P("dp", "expert", None),
        P("dp", "expert", None),
    )
    return jax.shard_map(
        on_device,
        mesh=mesh,
        in_specs=placed,
        out_specs=(
            P("dp", "expert", None),
            P("expert", "dp", None, None),
            P("expert", "dp", None),
            P("dp", "expert", None),
        ),
        check_vma=False,
    )
```

```python
import jax
import jax.numpy as jnp
from jax import lax
from jax.sharding import PartitionSpec as P

CHUNKS = 4


def slot_ranks(choices, experts):
    flat = choices.reshape(-1)
    onehot = (flat[:, None] == jnp.arange(experts, dtype=jnp.int32)[None, :]).astype(jnp.int32)
    earlier = jnp.cumsum(onehot, axis=0) - onehot
    return jnp.sum(earlier * onehot, axis=1).reshape(choices.shape)


def on_device(hidden, w_down, expert_ids, route_weights, grad_out):
    experts = lax.axis_size("expert")
    groups = lax.axis_size("dp")
    assert groups == 4
    slots = hidden.shape[2] // experts
    width = w_down.shape[2]
    kpart = w_down.shape[1]
    f32, bf16 = jnp.float32, jnp.bfloat16
    d = lax.axis_index("dp")
    parity = d % 2
    half = d // 2
    mate = d + 1 - 2 * parity
    pair_a = [(i, i ^ 1) for i in range(groups)]
    pair_b = [(i, groups - 1 - i) for i in range(groups)]
    hid = hidden[0, 0]
    rows = hid.shape[0]

    def cols(x, k):
        return lax.dynamic_slice_in_dim(x, k * kpart, kpart, axis=1)

    hid_b = lax.ppermute(
        lax.dynamic_slice_in_dim(hid, (1 - half) * 2 * kpart, 2 * kpart, axis=1), "dp", pair_b
    )
    lhs_own = jnp.concatenate([cols(hid, d), cols(hid_b, parity)], axis=0)
    lhs_mate = jnp.concatenate([cols(hid, mate), cols(hid_b, 1 - parity)], axis=0)

    cw = width // CHUNKS
    w_whole = lax.all_gather(w_down, "dp", axis=1, tiled=True)[0]
    out_slots = jnp.dot(hid, w_whole, preferred_element_type=f32).astype(bf16)

    arrived = lax.all_to_all(
        out_slots.reshape(experts, slots, width), "expert", split_axis=0, concat_axis=0, tiled=True
    )
    arrived = arrived.reshape(experts * slots, width)
    choices = expert_ids[0]
    weights = route_weights[0]
    cotangent = grad_out[0].astype(f32)
    slot_rows = choices * slots + slot_ranks(choices, experts)
    out_pair = arrived[slot_rows].astype(f32)
    mixed = jnp.einsum("tk,tkd->td", weights, out_pair)
    d_route = jnp.einsum("td,tkd->tk", cotangent, out_pair)
    grad_pair = (weights[..., None] * cotangent[:, None, :]).astype(bf16)
    outgoing = jnp.zeros((experts * slots, width), bf16)
    outgoing = outgoing.at[slot_rows.reshape(-1)].set(grad_pair.reshape(-1, width))
    mine = lax.all_to_all(
        outgoing.reshape(experts, slots, width), "expert", split_axis=0, concat_axis=0, tiled=True
    )
    g_own = mine.reshape(experts * slots, width)

    d_hidden = jnp.einsum("rd,hd->rh", g_own, w_whole, preferred_element_type=f32).astype(bf16)
    g_own, _ = lax.optimization_barrier((g_own, out_slots))
    dw_c = []
    gb = got = None
    for c in range(CHUNKS):
        go = g_own[:, c * cw:(c + 1) * cw]
        if c:
            go, _ = lax.optimization_barrier((go, gb))
        gb = lax.ppermute(go, "dp", pair_b)
        g = jnp.concatenate([go, gb], axis=0)
        q_own = jnp.einsum("rh,rd->hd", lhs_own, g, preferred_element_type=f32)
        q_mate = jnp.einsum("rh,rd->hd", lhs_mate, g, preferred_element_type=f32)
        send = q_mate.astype(bf16)
        if c:
            send, _ = lax.optimization_barrier((send, got))
        got = lax.ppermute(send, "dp", pair_a)
        dw_c.append((q_own + got.astype(f32)).astype(bf16))
    d_weight = jnp.concatenate(dw_c, axis=1)

    return (
        mixed.astype(bf16)[None],
        d_hidden.reshape(hidden.shape),
        d_weight[None],
        d_route[None],
    )


def solution(mesh):
    placed = (
        P("expert", "dp", None, None),
        P("expert", "dp", None),
        P("dp", "expert", None),
        P("dp", "expert", None),
        P("dp", "expert", None),
    )
    return jax.shard_map(
        on_device,
        mesh=mesh,
        in_specs=placed,
        out_specs=(
            P("dp", "expert", None),
            P("expert", "dp", None, None),
            P("expert", "dp", None),
            P("dp", "expert", None),
        ),
        check_vma=False,
    )
```

```python
import jax
import jax.numpy as jnp
from jax import lax
from jax.sharding import PartitionSpec as P


def slot_ranks(choices, experts):
    flat = choices.reshape(-1)
    onehot = (flat[:, None] == jnp.arange(experts, dtype=jnp.int32)[None, :]).astype(jnp.int32)
    earlier = jnp.cumsum(onehot, axis=0) - onehot
    return jnp.sum(earlier * onehot, axis=1).reshape(choices.shape)


def on_device(hidden, w_down, expert_ids, route_weights, grad_out):
    experts = lax.axis_size("expert")
    groups = lax.axis_size("dp")
    slots = hidden.shape[2] // experts
    width = w_down.shape[2]
    w_whole = lax.all_gather(w_down, "dp", axis=1, tiled=True)[0]
    out_slots = jnp.dot(hidden[0, 0], w_whole, preferred_element_type=jnp.float32).astype(
        jnp.bfloat16
    )
    arrived = lax.all_to_all(
        out_slots.reshape(experts, slots, width), "expert", split_axis=0, concat_axis=0, tiled=True
    )
    arrived = arrived.reshape(experts * slots, width)
    choices = expert_ids[0]
    weights = route_weights[0]
    cotangent = grad_out[0].astype(jnp.float32)
    rows = choices * slots + slot_ranks(choices, experts)
    out_pair = arrived[rows].astype(jnp.float32)
    mixed = jnp.einsum("tk,tkd->td", weights, out_pair)
    d_route = jnp.einsum("td,tkd->tk", cotangent, out_pair)
    grad_pair = (weights[..., None] * cotangent[:, None, :]).astype(jnp.bfloat16)
    outgoing = jnp.zeros((experts * slots, width), jnp.bfloat16)
    outgoing = outgoing.at[rows.reshape(-1)].set(grad_pair.reshape(-1, width))
    mine = lax.all_to_all(
        outgoing.reshape(experts, 1, slots, width),
        "expert",
        split_axis=0,
        concat_axis=0,
        tiled=True,
    )
    own_grads = mine[:, 0]
    d_hidden = jnp.einsum(
        "rd,hd->rh", own_grads.reshape(-1, width), w_whole, preferred_element_type=jnp.float32
    ).astype(jnp.bfloat16)
    columns = lax.all_to_all(hidden, "dp", split_axis=3, concat_axis=1, tiled=True)[0]
    columns = columns.reshape(groups, experts, slots, columns.shape[-1])
    cw = width // 2
    parts = []
    for c in range(2):
        slot_grads = lax.all_gather(mine[..., c * cw:(c + 1) * cw], "dp", axis=1, tiled=True)
        parts.append(jnp.einsum(
            "gsch,sgcd->hd", columns, slot_grads, preferred_element_type=jnp.float32
        ).astype(jnp.bfloat16))
    d_weight = jnp.concatenate(parts, axis=1)
    return (
        mixed.astype(jnp.bfloat16)[None],
        d_hidden.reshape(hidden.shape),
        d_weight[None],
        d_route[None],
    )


def solution(mesh):
    placed = (
        P("expert", "dp", None, None),
        P("expert", "dp", None),
        P("dp", "expert", None),
        P("dp", "expert", None),
        P("dp", "expert", None),
    )
    return jax.shard_map(
        on_device,
        mesh=mesh,
        in_specs=placed,
        out_specs=(
            P("dp", "expert", None),
            P("expert", "dp", None, None),
            P("expert", "dp", None),
            P("dp", "expert", None),
        ),
        check_vma=False,
    )
```

```python
import jax
import jax.numpy as jnp
from jax import lax
from jax.sharding import PartitionSpec as P

CHUNKS = 4


def slot_ranks(choices, experts):
    flat = choices.reshape(-1)
    onehot = (flat[:, None] == jnp.arange(experts, dtype=jnp.int32)[None, :]).astype(jnp.int32)
    earlier = jnp.cumsum(onehot, axis=0) - onehot
    return jnp.sum(earlier * onehot, axis=1).reshape(choices.shape)


def on_device(hidden, w_down, expert_ids, route_weights, grad_out):
    experts = lax.axis_size("expert")
    groups = lax.axis_size("dp")
    assert groups == 4
    slots = hidden.shape[2] // experts
    width = w_down.shape[2]
    kpart = w_down.shape[1]
    f32, bf16 = jnp.float32, jnp.bfloat16
    d = lax.axis_index("dp")
    parity = d % 2
    half = d // 2
    mate = d + 1 - 2 * parity
    pair_a = [(i, i ^ 1) for i in range(groups)]
    pair_b = [(i, groups - 1 - i) for i in range(groups)]
    hid = hidden[0, 0]
    rows = hid.shape[0]

    def cols(x, k):
        return lax.dynamic_slice_in_dim(x, k * kpart, kpart, axis=1)

    hid_b = lax.ppermute(
        lax.dynamic_slice_in_dim(hid, (1 - half) * 2 * kpart, 2 * kpart, axis=1), "dp", pair_b
    )
    lhs_own = jnp.concatenate([cols(hid, d), cols(hid_b, parity)], axis=0)
    lhs_mate = jnp.concatenate([cols(hid, mate), cols(hid_b, 1 - parity)], axis=0)

    cw = width // CHUNKS
    w_whole = lax.all_gather(w_down, "dp", axis=1, tiled=True)[0]
    out_slots = jnp.dot(hid, w_whole, preferred_element_type=f32).astype(bf16)

    arrived = lax.all_to_all(
        out_slots.reshape(experts, slots, width), "expert", split_axis=0, concat_axis=0, tiled=True
    )
    arrived = arrived.reshape(experts * slots, width)
    choices = expert_ids[0]
    weights = route_weights[0]
    cotangent = grad_out[0].astype(f32)
    slot_rows = choices * slots + slot_ranks(choices, experts)
    out_pair = arrived[slot_rows].astype(f32)
    mixed = jnp.einsum("tk,tkd->td", weights, out_pair)
    d_route = jnp.einsum("td,tkd->tk", cotangent, out_pair)
    grad_pair = (weights[..., None] * cotangent[:, None, :]).astype(bf16)
    outgoing = jnp.zeros((experts * slots, width), bf16)
    outgoing = outgoing.at[slot_rows.reshape(-1)].set(grad_pair.reshape(-1, width))
    mine = lax.all_to_all(
        outgoing.reshape(experts, slots, width), "expert", split_axis=0, concat_axis=0, tiled=True
    )
    g_own = mine.reshape(experts * slots, width)

    d_hidden = jnp.einsum("rd,hd->rh", g_own, w_whole, preferred_element_type=f32).astype(bf16)
    cw = width // CHUNKS
    split = width // 2
    columns = lax.all_to_all(hidden, "dp", split_axis=3, concat_axis=1, tiled=True)[0]
    columns = columns.reshape(groups, experts, slots, columns.shape[-1])
    slot_grads = lax.all_gather(
        mine.reshape(experts, 1, slots, width)[..., :split], "dp", axis=1, tiled=True
    )
    dw_c = [jnp.einsum(
        "gsch,sgcd->hd", columns, slot_grads, preferred_element_type=f32
    ).astype(bf16)]
    g_own, _ = lax.optimization_barrier((g_own, out_slots))
    gb = got = None
    for c in range(split // cw, CHUNKS):
        go = g_own[:, c * cw:(c + 1) * cw]
        if gb is not None:
            go, _ = lax.optimization_barrier((go, gb))
        gb = lax.ppermute(go, "dp", pair_b)
        g = jnp.concatenate([go, gb], axis=0)
        q_own = jnp.einsum("rh,rd->hd", lhs_own, g, preferred_element_type=f32)
        q_mate = jnp.einsum("rh,rd->hd", lhs_mate, g, preferred_element_type=f32)
        send = q_mate.astype(bf16)
        if got is not None:
            send, _ = lax.optimization_barrier((send, got))
        got = lax.ppermute(send, "dp", pair_a)
        dw_c.append((q_own + got.astype(f32)).astype(bf16))
    d_weight = jnp.concatenate(dw_c, axis=1)

    return (
        mixed.astype(bf16)[None],
        d_hidden.reshape(hidden.shape),
        d_weight[None],
        d_route[None],
    )


def solution(mesh):
    placed = (
        P("expert", "dp", None, None),
        P("expert", "dp", None),
        P("dp", "expert", None),
        P("dp", "expert", None),
        P("dp", "expert", None),
    )
    return jax.shard_map(
        on_device,
        mesh=mesh,
        in_specs=placed,
        out_specs=(
            P("dp", "expert", None),
            P("expert", "dp", None, None),
            P("expert", "dp", None),
            P("dp", "expert", None),
        ),
        check_vma=False,
    )
```

```python
import jax
import jax.numpy as jnp
from jax import lax
from jax.sharding import PartitionSpec as P
from jax.experimental.layout import Layout, with_layout_constraint


def slot_ranks(choices, experts):
    flat = choices.reshape(-1)
    onehot = (flat[:, None] == jnp.arange(experts, dtype=jnp.int32)[None, :]).astype(jnp.int32)
    earlier = jnp.cumsum(onehot, axis=0) - onehot
    return jnp.sum(earlier * onehot, axis=1).reshape(choices.shape)


def on_device(hidden, w_down, expert_ids, route_weights, grad_out):
    experts = lax.axis_size("expert")
    groups = lax.axis_size("dp")
    slots = hidden.shape[2] // experts
    width = w_down.shape[2]
    w_whole = lax.all_gather(w_down, "dp", axis=1, tiled=True)[0]
    out_slots = jnp.dot(hidden[0, 0], w_whole, preferred_element_type=jnp.float32).astype(
        jnp.bfloat16
    )
    arrived = lax.all_to_all(
        out_slots.reshape(experts, slots, width), "expert", split_axis=0, concat_axis=0, tiled=True
    )
    arrived = arrived.reshape(experts * slots, width)
    choices = expert_ids[0]
    weights = route_weights[0]
    cotangent = grad_out[0].astype(jnp.float32)
    rows = choices * slots + slot_ranks(choices, experts)
    out_pair = arrived[rows].astype(jnp.float32)
    mixed = jnp.einsum("tk,tkd->td", weights, out_pair)
    d_route = jnp.einsum("td,tkd->tk", cotangent, out_pair)
    grad_pair = (weights[..., None] * cotangent[:, None, :]).astype(jnp.bfloat16)
    outgoing = jnp.zeros((experts * slots, width), jnp.bfloat16)
    outgoing = outgoing.at[rows.reshape(-1)].set(grad_pair.reshape(-1, width))
    mine = lax.all_to_all(
        outgoing.reshape(experts, 1, slots, width),
        "expert",
        split_axis=0,
        concat_axis=0,
        tiled=True,
    )
    own_grads = mine[:, 0]
    slot_grads = lax.all_gather(mine, "dp", axis=1, tiled=True)
    d_hidden = jnp.einsum(
        "rd,hd->rh", own_grads.reshape(-1, width), w_whole, preferred_element_type=jnp.float32
    ).astype(jnp.bfloat16)
    columns = lax.all_to_all(hidden, "dp", split_axis=3, concat_axis=1, tiled=True)[0]
    columns = columns.reshape(groups, experts, slots, columns.shape[-1])
    d_weight = jnp.einsum(
        "gsch,sgcd->hd", columns, slot_grads, preferred_element_type=jnp.float32
    ).astype(jnp.bfloat16)
    d_weight = with_layout_constraint(d_weight, Layout(major_to_minor=(0, 1)))
    return (
        mixed.astype(jnp.bfloat16)[None],
        d_hidden.reshape(hidden.shape),
        d_weight[None],
        d_route[None],
    )


def solution(mesh):
    placed = (
        P("expert", "dp", None, None),
        P("expert", "dp", None),
        P("dp", "expert", None),
        P("dp", "expert", None),
        P("dp", "expert", None),
    )
    return jax.shard_map(
        on_device,
        mesh=mesh,
        in_specs=placed,
        out_specs=(
            P("dp", "expert", None),
            P("expert", "dp", None, None),
            P("expert", "dp", None),
            P("dp", "expert", None),
        ),
        check_vma=False,
    )
```

```python
import jax
import jax.numpy as jnp
from jax import lax
from jax.sharding import PartitionSpec as P
from jax.experimental.layout import Layout, with_layout_constraint


def slot_ranks(choices, experts):
    flat = choices.reshape(-1)
    onehot = (flat[:, None] == jnp.arange(experts, dtype=jnp.int32)[None, :]).astype(jnp.int32)
    earlier = jnp.cumsum(onehot, axis=0) - onehot
    return jnp.sum(earlier * onehot, axis=1).reshape(choices.shape)


def on_device(hidden, w_down, expert_ids, route_weights, grad_out):
    experts = lax.axis_size("expert")
    groups = lax.axis_size("dp")
    slots = hidden.shape[2] // experts
    width = w_down.shape[2]
    w_whole = lax.all_gather(w_down, "dp", axis=1, tiled=True)[0]
    out_slots = jnp.dot(hidden[0, 0], w_whole, preferred_element_type=jnp.float32).astype(
        jnp.bfloat16
    )
    arrived = lax.all_to_all(
        out_slots.reshape(experts, slots, width), "expert", split_axis=0, concat_axis=0, tiled=True
    )
    arrived = arrived.reshape(experts * slots, width)
    choices = expert_ids[0]
    weights = route_weights[0]
    cotangent = grad_out[0].astype(jnp.float32)
    rows = choices * slots + slot_ranks(choices, experts)
    out_pair = arrived[rows].astype(jnp.float32)
    mixed = jnp.einsum("tk,tkd->td", weights, out_pair)
    d_route = jnp.einsum("td,tkd->tk", cotangent, out_pair)
    grad_pair = (weights[..., None] * cotangent[:, None, :]).astype(jnp.bfloat16)
    outgoing = jnp.zeros((experts * slots, width), jnp.bfloat16)
    outgoing = outgoing.at[rows.reshape(-1)].set(grad_pair.reshape(-1, width))
    mine = lax.all_to_all(
        outgoing.reshape(experts, 1, slots, width),
        "expert",
        split_axis=0,
        concat_axis=0,
        tiled=True,
    )
    own_grads = mine[:, 0]
    slot_grads = lax.all_gather(mine, "dp", axis=1, tiled=True)
    slot_grads = with_layout_constraint(slot_grads, Layout(major_to_minor=(1, 0, 2, 3)))
    d_hidden = jnp.einsum(
        "rd,hd->rh", own_grads.reshape(-1, width), w_whole, preferred_element_type=jnp.float32
    ).astype(jnp.bfloat16)
    columns = lax.all_to_all(hidden, "dp", split_axis=3, concat_axis=1, tiled=True)[0]
    columns = columns.reshape(groups, experts, slots, columns.shape[-1])
    d_weight = jnp.einsum(
        "gsch,sgcd->hd", columns, slot_grads, preferred_element_type=jnp.float32
    ).astype(jnp.bfloat16)
    d_weight = with_layout_constraint(d_weight, Layout(major_to_minor=(0, 1)))
    return (
        mixed.astype(jnp.bfloat16)[None],
        d_hidden.reshape(hidden.shape),
        d_weight[None],
        d_route[None],
    )


def solution(mesh):
    placed = (
        P("expert", "dp", None, None),
        P("expert", "dp", None),
        P("dp", "expert", None),
        P("dp", "expert", None),
        P("dp", "expert", None),
    )
    return jax.shard_map(
        on_device,
        mesh=mesh,
        in_specs=placed,
        out_specs=(
            P("dp", "expert", None),
            P("expert", "dp", None, None),
            P("expert", "dp", None),
            P("dp", "expert", None),
        ),
        check_vma=False,
    )
```
